32 devices in a mesh: dp: 4 (over y, core), ha: 2 (over x), wa: 4 (over z).
Axes of the slice: x: 2, y: 2, z: 4, core: 2. Of those that a mesh axis runs over, the one named last changes fastest.
Arguments:
- features: bfloat16 [4, 8, 16, 1536], P('dp', 'ha', 'wa'), may hold values from -6 to 6
- out_grads: bfloat16 [4, 8, 16, 1536], P('dp', 'ha', 'wa'), may hold values from -6 to 6
- conv_kernel: bfloat16 [49, 1536], replicated, may hold values from -0.875 to 0.875
- conv_bias: float32 [1536], replicated, may hold values from -3 to 3
- norm_gain: float32 [1536], replicated, may hold values from 0.25 to 1.75
- norm_shift: float32 [1536], replicated, may hold values from -3 to 3
- up_weight: bfloat16 [1536, 6144], P(('dp', 'ha'), 'wa'), may hold values from -0.15625 to 0.15625
- up_bias: float32 [6144], P('wa'), may hold values from -3 to 3
- down_weight: bfloat16 [6144, 1536], P('wa', ('dp', 'ha')), may hold values from -0.078125 to 0.078125
- layer_scale: float32 [1536], replicated, may hold values from 0.25 to 2
Outputs:
- input_grad: bfloat16 [4, 8, 16, 1536], P('dp', 'ha', 'wa')
- up_weight_grad: float32 [1536, 6144], P(('dp', 'ha'), 'wa')
- down_weight_grad: float32 [6144, 1536], P('wa', ('dp', 'ha'))
The draws below stay inside these ranges and needn't reach their ends.
All inputs are finite; a program needn't handle non-finite values.
Results may differ from the reference program's by a relative error of at most 0.01.
Values may be sent and summed in bfloat16 or wider, within the bound.
No kernel may reach another device: no remote copies, remote signals or barrier semaphores. Data moves between devices by JAX's collectives and lax.ppermute only.
A program may use at most 64 MiB of HBM per device.

```python
import math
import jax
import jax.numpy as jnp
from jax import lax

CH = 1536
FF = 6144
IMG_DEV = 1
ROWS_DEV = 4
IMAGES = 4
MAP_H = 8
MAP_W = 16
N_DP = 4
N_HA = 2
N_WA = 4


def level_of(key, shape, split, smallest, top_value):
    factor_of, own = 1.0, jax.random.fold_in(key, 6)
    for position, parts in split:
        steps = jnp.exp(jax.random.uniform(jax.random.fold_in(own, position), (parts,), jnp.float32, smallest / len(split), top_value / len(split)))
        factor_of = factor_of * jnp.repeat(steps, shape[position] // parts).reshape([-1 if axis == position else 1 for axis in range(len(shape))])
    return factor_of


def normal_values(stream_key, extent, deviation, bound, cuts=(), kind=jnp.bfloat16):
    array = jax.random.normal(stream_key, extent, jnp.float32) * deviation
    if len(cuts) > 0:
        array = level_of(stream_key, extent, cuts, -0.22, 0.18) * array
    return jnp.clip(array, min=-bound, max=bound).astype(kind)


def setup_inputs(seed: int = 0) -> dict:
    splits = jax.random.split(jax.random.key(seed), 11)
    features = normal_values(splits[0], (IMAGES, MAP_H, MAP_W, CH), 1.0, 6.0, ((0, 4), (1, 2), (2, 4)))
    out_grads = normal_values(splits[1], (IMAGES, MAP_H, MAP_W, CH), 1.0, 6.0, ((0, 4), (1, 2), (2, 4)))
    conv_kernel = normal_values(splits[2], (49, CH), 49 ** -0.5, 0.875)
    conv_bias = normal_values(splits[3], (CH,), 0.5, 3.0, (), jnp.float32)
    norm_gain = jnp.clip(1.0 + 0.15 * jax.random.normal(splits[4], (CH,), jnp.float32), 0.25, 1.75)
    norm_shift = normal_values(splits[5], (CH,), 0.5, 3.0, (), jnp.float32)
    up_weight = normal_values(splits[6], (CH, FF), CH ** -0.5, 0.15625, ((0, 8), (1, 4)))
    up_bias = normal_values(splits[7], (FF,), 0.5, 3.0, ((0, 4),), jnp.float32)
    down_weight = normal_values(splits[8], (FF, CH), FF ** -0.5, 0.078125, ((0, 4), (1, 8)))
    layer_scale = jnp.clip(jnp.exp(jax.random.uniform(splits[9], (CH,), jnp.float32, math.log(0.25), math.log(2.0))), 0.25, 2.0)
    return dict(features=features, out_grads=out_grads, conv_kernel=conv_kernel, conv_bias=conv_bias, norm_gain=norm_gain, norm_shift=norm_shift, up_weight=up_weight, up_bias=up_bias, down_weight=down_weight, layer_scale=layer_scale)


EPSILON = 1e-06
HALF_ROOT = 0.7071067811865476
DENSITY_SCALE = 0.3989422804014327

def depthwise(padded, kernel_f, row_count, col_count, flipped):
    summed = jnp.zeros(padded.shape[:1] + (row_count, col_count) + padded.shape[3:], jnp.float32)
    for tap_index in range(49):
        row_off = tap_index // 7
        col_off = tap_index % 7
        if flipped:
            row_off = 6 - row_off
            col_off = 6 - col_off
        window = padded[:, row_off:row_off + row_count, col_off:col_off + col_count, :]
        summed = summed + window.astype(jnp.float32) * kernel_f[tap_index]
    return summed

def norm_forward(summed, norm_gain, norm_shift):
    center = lax.optimization_barrier(jnp.mean(summed, axis=-1, keepdims=True))
    deviate = summed - center
    inv_scale = lax.rsqrt(lax.optimization_barrier(jnp.mean(deviate * deviate, axis=-1, keepdims=True)) + EPSILON)
    normed = deviate * inv_scale
    return (normed, inv_scale, (normed * norm_gain + norm_shift).astype(jnp.bfloat16))

def grouped(values_in):
    trailing = values_in.shape[-1]
    shaped = values_in.reshape(N_DP, IMG_DEV, N_HA, ROWS_DEV, MAP_W, trailing)
    return shaped.transpose(0, 2, 1, 3, 4, 5).reshape(N_DP * N_HA, IMG_DEV * ROWS_DEV * MAP_W, trailing)

def ungrouped(values_in):
    trailing = values_in.shape[-1]
    shaped = values_in.reshape(N_DP, N_HA, IMG_DEV, ROWS_DEV, MAP_W, trailing)
    return shaped.transpose(0, 2, 1, 3, 4, 5).reshape(IMAGES, MAP_H, MAP_W, trailing)

def reference(features, out_grads, conv_kernel, conv_bias, norm_gain, norm_shift, up_weight, up_bias, down_weight, layer_scale):
    kernel_f = conv_kernel.astype(jnp.float32)
    padded = jnp.pad(features, ((0, 0), (3, 3), (3, 3), (0, 0)))
    summed = depthwise(padded, kernel_f, MAP_H, MAP_W, False) + conv_bias
    normed, inv_scale, normed_out = norm_forward(summed, norm_gain, norm_shift)
    scaled = (out_grads.astype(jnp.float32) * layer_scale).astype(jnp.bfloat16)
    up_split = up_weight.astype(jnp.float32).reshape(CH, N_WA, FF // N_WA)

    def group_step(running, group_pair):
        rows_in, rows_grad = group_pair
        hidden_pre = jnp.dot(rows_in, up_weight, preferred_element_type=jnp.float32) + up_bias
        normal_cdf = 0.5 * (1.0 + lax.erf(hidden_pre * HALF_ROOT))
        activated = (hidden_pre * normal_cdf).astype(jnp.bfloat16)
        gelu_slope = normal_cdf + hidden_pre * DENSITY_SCALE * jnp.exp(-0.5 * hidden_pre * hidden_pre)
        act_grad = lax.dot_general(rows_grad, down_weight, (((1,), (1,)), ((), ())), preferred_element_type=jnp.float32)
        pre_grad = (act_grad * gelu_slope).astype(jnp.bfloat16)
        up_term = lax.dot_general(rows_in, pre_grad, (((0,), (0,)), ((), ())), preferred_element_type=jnp.float32)
        down_term = lax.dot_general(activated, rows_grad, (((0,), (0,)), ((), ())), preferred_element_type=jnp.float32)
        up_term = lax.optimization_barrier(up_term.astype(jnp.bfloat16)).astype(jnp.float32)
        down_term = lax.optimization_barrier(down_term.astype(jnp.bfloat16)).astype(jnp.float32)
        split_pre = pre_grad.astype(jnp.float32).reshape(-1, N_WA, FF // N_WA)
        split_terms = jnp.einsum('rgf,cgf->rgc', split_pre, up_split)
        split_terms = lax.optimization_barrier(split_terms.astype(jnp.bfloat16)).astype(jnp.float32)
        return ((running[0] + up_term, running[1] + down_term), lax.optimization_barrier(jnp.sum(split_terms, axis=1)))
    start_sums = (jnp.zeros((CH, FF), jnp.float32), jnp.zeros((FF, CH), jnp.float32))
    sums_out, norm_rows = lax.scan(group_step, start_sums, (grouped(normed_out), grouped(scaled)))
    norm_grad = ungrouped(norm_rows)
    scaled_grad = norm_grad * norm_gain
    center_grad = lax.optimization_barrier(jnp.mean(scaled_grad, axis=-1, keepdims=True))
    cross_mean = lax.optimization_barrier(jnp.mean(scaled_grad * normed, axis=-1, keepdims=True))
    summed_grad = (inv_scale * (scaled_grad - center_grad - normed * cross_mean)).astype(jnp.bfloat16)
    padded_grad = jnp.pad(summed_grad, ((0, 0), (3, 3), (3, 3), (0, 0)))
    input_grad = (out_grads.astype(jnp.float32) + depthwise(padded_grad, kernel_f, MAP_H, MAP_W, True)).astype(jnp.bfloat16)
    return (input_grad, sums_out[0], sums_out[1])
```

```python
import jax
import jax.numpy as jnp
from jax import lax
from jax.sharding import Mesh
from jax.sharding import PartitionSpec as P

EPSILON = 1e-06
HALF_ROOT = 0.7071067811865476
DENSITY_SCALE = 0.3989422804014327
CORES = 2
PLANE = ("y", "x")


def exchange(value, axes, count, step):
    return lax.ppermute(value, axes, [(i, i ^ step) for i in range(count)])


def halo(shard, axis, dim, width):
    count, length, index = lax.axis_size(axis), shard.shape[dim], lax.axis_index(axis)
    last = lax.slice_in_dim(shard, length - width, length, axis=dim)
    first = lax.slice_in_dim(shard, 0, width, axis=dim)
    even = index % 2 == 0
    outer = [(i, i ^ 1) for i in range(count)]
    got_a = lax.ppermute(jnp.where(even, last, first), axis, outer)
    if count == 2:
        got_b = jnp.zeros_like(got_a)
    else:
        inner = [(i, ((i + 1) ^ 1) - 1) for i in range(1, count - 1)]
        got_b = lax.ppermute(jnp.where(even, first, last), axis, inner)
    before = jnp.where(even, got_b, got_a)
    after = jnp.where(even, got_a, got_b)
    return jnp.concatenate([before, shard, after], axis=dim)


def depthwise(padded, kernel_f, row_count, col_count, flipped):
    summed = jnp.zeros(padded.shape[:1] + (row_count, col_count) + padded.shape[3:], jnp.float32)
    for tap_index in range(49):
        row_off = tap_index // 7
        col_off = tap_index % 7
        if flipped:
            row_off = 6 - row_off
            col_off = 6 - col_off
        window = padded[:, row_off : row_off + row_count, col_off : col_off + col_count, :]
        summed = summed + window.astype(jnp.float32) * kernel_f[tap_index]
    return summed


def norm_forward(summed, norm_gain, norm_shift):
    center = jnp.mean(summed, axis=-1, keepdims=True)
    deviate = summed - center
    inv_scale = lax.rsqrt(jnp.mean(deviate * deviate, axis=-1, keepdims=True) + EPSILON)
    normed = deviate * inv_scale
    return (normed, inv_scale, (normed * norm_gain + norm_shift).astype(jnp.bfloat16))


def gathered(value, axes, count):
    return [value] + [exchange(value, axes, count, k) for k in range(1, count)]


def contract(a, b, dims):
    return lax.dot_general(a, b, (dims, ((), ())), preferred_element_type=jnp.float32)


def body(
    features,
    out_grads,
    conv_kernel,
    conv_bias,
    norm_gain,
    norm_shift,
    up_weight,
    up_bias,
    down_weight,
    layer_scale,
):
    images, band_rows, tile_cols, channels = features.shape
    tokens = images * band_rows * tile_cols
    ny, nx, nz = lax.axis_size("y"), lax.axis_size("x"), lax.axis_size("z")
    chips = ny * nx
    y, core, x = lax.axis_index("y"), lax.axis_index("c"), lax.axis_index("x")
    chip = y * nx + x
    rows, hidden = up_weight.shape
    part = hidden // chips
    kernel_f = conv_kernel.astype(jnp.float32)

    stacked = jnp.stack([up_weight, down_weight.T])

    def columns(owner):
        return lax.dynamic_slice_in_dim(stacked, owner * part, part, axis=2)

    pieces = [columns(chip)]
    pieces += [exchange(columns(chip ^ k), PLANE, chips, k) for k in range(1, chips)]
    mine = jnp.stack(pieces)
    other = exchange(mine, "c", CORES, 1)

    padded = halo(halo(features, "x", 1, 3), "z", 2, 3)
    summed = depthwise(padded, kernel_f, band_rows, tile_cols, False) + conv_bias
    normed, inv_scale, normed_out = norm_forward(summed, norm_gain, norm_shift)

    scaled = (out_grads.astype(jnp.float32) * layer_scale).astype(jnp.bfloat16)
    scaled_z = jnp.concatenate(gathered(scaled.reshape(tokens, channels), "z", nz))
    scaled_rows = jnp.concatenate(gathered(scaled_z, PLANE, chips))
    normed_z = jnp.concatenate(gathered(normed_out.reshape(tokens, channels), "z", nz))
    normed_rows = jnp.concatenate(gathered(normed_z, PLANE, chips))

    by_core = jnp.where(core == 0, jnp.stack([mine, other]), jnp.stack([other, mine]))
    order = jnp.stack([chip ^ p for p in range(chips)])
    by_owner = jnp.take(by_core, order, axis=1)
    by_owner = by_owner.reshape(CORES, ny, nx, 2, rows, part).transpose(3, 1, 0, 2, 4, 5)
    by_owner = by_owner.reshape(2, channels, part)
    up_part, down_part = by_owner[0], by_owner[1]

    bias = lax.dynamic_slice_in_dim(up_bias, chip * part, part)
    hidden_pre = contract(normed_rows, up_part, ((1,), (0,))) + bias
    normal_cdf = 0.5 * (1.0 + lax.erf(hidden_pre * HALF_ROOT))
    activated = (hidden_pre * normal_cdf).astype(jnp.bfloat16)
    gelu_slope = normal_cdf + hidden_pre * DENSITY_SCALE * jnp.exp(-0.5 * hidden_pre * hidden_pre)
    act_grad = contract(scaled_rows, down_part, ((1,), (0,)))
    pre_grad = (act_grad * gelu_slope).astype(jnp.bfloat16)

    norm_part = contract(pre_grad, up_part, ((1,), (1,))).astype(jnp.bfloat16)
    norm_part = norm_part.reshape(chips, nz * tokens, channels)
    total = norm_part[0].astype(jnp.float32)
    for k in range(1, chips):
        total = total + exchange(norm_part[k], PLANE, chips, k).astype(jnp.float32)
    norm_part = total.astype(jnp.bfloat16).reshape(nz, tokens, channels)
    total = norm_part[0].astype(jnp.float32)
    for k in range(1, nz):
        total = total + exchange(norm_part[k], "z", nz, k).astype(jnp.float32)
    norm_grad = total.reshape(images, band_rows, tile_cols, channels)
    scaled_grad = norm_grad * norm_gain
    center_grad = jnp.mean(scaled_grad, axis=-1, keepdims=True)
    cross_mean = jnp.mean(scaled_grad * normed, axis=-1, keepdims=True)
    summed_grad = (inv_scale * (scaled_grad - center_grad - normed * cross_mean)).astype(
        jnp.bfloat16
    )
    padded_grad = halo(halo(summed_grad, "x", 1, 3), "z", 2, 3)
    conv_grad = depthwise(padded_grad, kernel_f, band_rows, tile_cols, True)
    input_grad = (out_grads.astype(jnp.float32) + conv_grad).astype(jnp.bfloat16)

    grads = jnp.stack(
        [
            contract(normed_rows, pre_grad, ((0,), (0,))),
            contract(scaled_rows, activated, ((0,), (0,))),
        ]
    ).astype(jnp.bfloat16)
    grads = grads.reshape(2, ny, CORES, nx, rows, part).transpose(2, 1, 3, 0, 4, 5)
    grads = grads.reshape(CORES, chips, 2, rows, part)
    keep = lax.dynamic_index_in_dim(grads, core, 0, keepdims=False)
    give = lax.dynamic_index_in_dim(grads, 1 - core, 0, keepdims=False)
    sums = keep.astype(jnp.float32) + exchange(give, "c", CORES, 1).astype(jnp.float32)
    sums = sums.astype(jnp.bfloat16)

    def owned(owner):
        return lax.dynamic_index_in_dim(sums, owner, 0, keepdims=False)

    shares = [owned(chip)] + [exchange(owned(chip ^ k), PLANE, chips, k) for k in range(1, chips)]
    shares = jnp.take(jnp.stack(shares), order, axis=0)
    shares = shares.transpose(1, 2, 0, 3).reshape(2, rows, hidden).astype(jnp.float32)
    return (input_grad, shares[0], shares[1].T)


def solution(mesh):
    n_dp, nx, nz = (mesh.shape[name] for name in ("dp", "ha", "wa"))
    split = Mesh(mesh.devices.reshape(n_dp // CORES, CORES, nx, nz), ("y", "c", "x", "z"))
    dp, owners = ("y", "c"), ("y", "c", "x")
    image = P(dp, "x", "z", None)
    return jax.shard_map(
        body,
        mesh=split,
        in_specs=(
            image,
            image,
            P(),
            P(),
            P(),
            P(),
            P(owners, "z"),
            P("z"),
            P("z", owners),
            P(),
        ),
        out_specs=(image, P(owners, "z"), P("z", owners)),
        check_vma=False,
    )
```
